256 devices in a mesh: dp: 4 (over x_hi, core), ctx: 64 (over y, z, x_lo).
Axes of the slice: x: 4 (x_hi: 2, x_lo: 2; x = x_hi * 2 + x_lo), y: 4, z: 8, core: 2. Of those that a mesh axis runs over, the one named last changes fastest.
Arguments:
- frames: bfloat16 [4, 12288, 1024], P('dp', 'ctx'), may hold values from -60 to 60
- lengths: int32 [4], P('dp'), may hold values from 6144 to 12288, as said below
- w_qkv: bfloat16 [1024, 1536], replicated, may hold values from -0.9 to 0.9
- w_out: bfloat16 [512, 1024], replicated, may hold values from -0.25 to 0.25
- w_pw1: bfloat16 [1024, 2048], replicated, may hold values from -0.1875 to 0.1875
- conv_taps: float32 [31, 1024], replicated, may hold values from -1 to 1
- w_pw2: bfloat16 [1024, 1024], replicated, may hold values from -0.1875 to 0.1875
Outputs:
- encoded: bfloat16 [4, 12288, 1024], P('dp', 'ctx')
The draws below stay inside these ranges and needn't reach their ends.
Inputs may be any that keep to these rules, and one draw needn't show every extreme that they name: `lengths`: the valid frames of a recording are its first ones; some recording has all 12288 frames valid.
All inputs are finite; a program needn't handle non-finite values.
Results may differ from the reference program's by a relative error of at most 0.011.
Values may be sent and summed in bfloat16 or wider, within the bound.
A program may use at most 256 MiB of HBM per device.

```python
import math
import jax
import jax.numpy as jnp
from jax import lax

D = 1024
HEADS = 8
HEAD_DIM = 64
KW = 31
FR_DEV = 192
FRAMES = 12288
HD = 512
N_DP = 4
N_CTX = 64


def draw_frames(key, part):
    shape = (N_DP, FRAMES, D)
    key_row, key_col, key_base = jax.random.split(jax.random.fold_in(key, 11), 3)
    row_scale = jnp.exp(jax.random.uniform(key_row, (N_DP, FRAMES, 1), minval=math.log(0.3), maxval=math.log(3.0)))
    col_scale = jnp.exp(jax.random.uniform(key_col, (N_DP, 1, D), minval=math.log(0.3), maxval=math.log(3.0)))
    noise = jnp.clip(jax.random.normal(key_base, shape), -5.0, 5.0)
    return jnp.clip(noise * row_scale * col_scale, -60.0, 60.0).astype(jnp.bfloat16)


def draw_lengths(key, part):
    drawn = jax.random.randint(jax.random.fold_in(key, 23), (N_DP,), FRAMES // 2, FRAMES + 1)
    return drawn.at[0].set(FRAMES)


def draw_w_qkv(key, part):
    deviation = 2.0 / math.sqrt(D)
    key_main = jax.random.fold_in(key, 37)
    raw = jnp.clip(jax.random.normal(key_main, (D, 3 * HD)), -5.0, 5.0) * deviation
    return jnp.clip(raw, -0.9, 0.9).astype(jnp.bfloat16)


def centred(stream_key, shape, scale, bound, kind=jnp.bfloat16):
    result = scale * jax.random.normal(stream_key, shape, jnp.float32)
    return jnp.clip(result, min=-bound, max=bound).astype(kind)


def setup_inputs(seed: int = 0) -> dict:
    seeds = jax.random.split(jax.random.key(seed), 8)
    frames = draw_frames(jax.random.fold_in(seeds[7], 71), 0)
    lengths = draw_lengths(jax.random.fold_in(seeds[7], 71), 0)
    w_qkv = draw_w_qkv(jax.random.fold_in(seeds[7], 71), 0)
    w_out = centred(seeds[3], (HD, D), HD ** -0.5, 0.25)
    w_pw1 = centred(seeds[4], (D, 2 * D), D ** -0.5, 0.1875)
    conv_taps = centred(seeds[5], (KW, D), KW ** -0.5, 1.0, jnp.float32)
    w_pw2 = centred(seeds[6], (D, D), D ** -0.5, 0.1875)
    return {"frames": frames, "lengths": lengths, "w_qkv": w_qkv, "w_out": w_out, "w_pw1": w_pw1, "conv_taps": conv_taps, "w_pw2": w_pw2}


epsilon = 1e-05
masked_score = -1e+30

def to_bf16(value):
    return lax.optimization_barrier(value.astype(jnp.bfloat16))

def layer_norm(value):
    center = value - lax.optimization_barrier(jnp.mean(value, axis=-1, keepdims=True))
    spread = lax.optimization_barrier(jnp.mean(center * center, axis=-1, keepdims=True))
    return center * lax.rsqrt(spread + epsilon)

def depthwise(padded, conv_taps, count):
    total = jnp.zeros((count, padded.shape[1]), jnp.float32)
    for tap_index in range(conv_taps.shape[0]):
        total = total + conv_taps[tap_index] * padded[tap_index:tap_index + count].astype(jnp.float32)
    return total

def one_recording(stream, limit, w_qkv, w_out, w_pw1, conv_taps, w_pw2):
    positions = jnp.arange(FRAMES, dtype=jnp.int32)
    valid = positions < limit
    normed = to_bf16(layer_norm(stream.astype(jnp.float32)))
    projected = jnp.dot(normed, w_qkv, preferred_element_type=jnp.float32)
    queries = to_bf16(projected[:, :HD] * HEAD_DIM ** (-0.5))
    keys = to_bf16(projected[:, HD:2 * HD]).astype(jnp.float32).reshape(FRAMES, HEADS, HEAD_DIM)
    values = to_bf16(projected[:, 2 * HD:]).astype(jnp.float32).reshape(FRAMES, HEADS, HEAD_DIM)
    query_blocks = queries.reshape(N_CTX, FR_DEV, HEADS, HEAD_DIM)

    def attend(block):
        scores = jnp.einsum('qhd,khd->hqk', block.astype(jnp.float32), keys)
        masked = jnp.where(valid, scores, masked_score)
        largest = lax.optimization_barrier(jnp.max(masked, axis=-1, keepdims=True))
        weights = jnp.where(valid, jnp.exp(masked - largest), 0.0)
        totals = lax.optimization_barrier(jnp.sum(weights, axis=-1))
        mixed = jnp.einsum('hqk,khd->qhd', to_bf16(weights).astype(jnp.float32), values)
        return to_bf16(mixed / totals.T[:, :, None]).reshape(FR_DEV, HD)
    attended = lax.map(attend, query_blocks).reshape(FRAMES, HD)
    first = to_bf16(stream.astype(jnp.float32) + jnp.dot(attended, w_out, preferred_element_type=jnp.float32))
    gated = jnp.dot(to_bf16(layer_norm(first.astype(jnp.float32))), w_pw1, preferred_element_type=jnp.float32)
    glu = gated[:, :D] * jax.nn.sigmoid(gated[:, D:])
    glu = to_bf16(jnp.where(valid[:, None], glu, 0.0))
    half_width = KW // 2
    padded = jnp.pad(glu, ((half_width, half_width), (0, 0)))
    conv = depthwise(padded, conv_taps, FRAMES)
    swished = to_bf16(jax.nn.silu(layer_norm(conv)))
    second = first.astype(jnp.float32) + jnp.dot(swished, w_pw2, preferred_element_type=jnp.float32)
    return jnp.where(valid[:, None], layer_norm(second), 0.0).astype(jnp.bfloat16)

def reference(frames, lengths, w_qkv, w_out, w_pw1, conv_taps, w_pw2):
    outputs = []
    for record in range(N_DP):
        outputs.append(one_recording(frames[record], lengths[record], w_qkv, w_out, w_pw1, conv_taps, w_pw2))
    return jnp.stack(outputs)
```

```python
import jax
import jax.numpy as jnp
from jax import lax
from jax.experimental import pallas as pl
from jax.experimental.pallas import tpu as pltpu
from jax.sharding import PartitionSpec as P

HEADS = 8


epsilon = 1e-05
masked_score = -1e30


def padded_2(cells, sides, width):
    for axis, dim in sides:
        count = lax.axis_size(axis)
        ends = count - 1
        head = lax.slice_in_dim(cells, 0, width, axis=dim)
        tail = lax.slice_in_dim(cells, cells.shape[dim] - width, cells.shape[dim], axis=dim)
        cells = jnp.concatenate(
            [
                lax.ppermute(tail, axis, [(i, (i + 1) % count) for i in range(ends)]),
                cells,
                lax.ppermute(head, axis, [((i + 1) % count, i) for i in range(ends)]),
            ],
            axis=dim,
        )
    return cells


def to_bf16(value):
    return value.astype(jnp.bfloat16)


def layer_norm(value):
    center = value - jnp.mean(value, axis=-1, keepdims=True)
    spread = jnp.mean(center * center, axis=-1, keepdims=True)
    return center * lax.rsqrt(spread + epsilon)


def depthwise(padded, conv_taps, count):
    total = jnp.zeros((count, padded.shape[1]), jnp.float32)
    for tap_index in range(conv_taps.shape[0]):
        total = total + conv_taps[tap_index] * padded[tap_index : tap_index + count].astype(
            jnp.float32
        )
    return total


def gate_rows(stream_rows, spots, limit, w_pw1):
    gated = jnp.dot(
        to_bf16(layer_norm(stream_rows.astype(jnp.float32))),
        w_pw1,
        preferred_element_type=jnp.float32,
    )
    half_cols = gated.shape[1] // 2
    result = gated[:, :half_cols] * jax.nn.sigmoid(gated[:, half_cols:])
    return to_bf16(jnp.where((spots < limit)[:, None], result, 0.0))


def attend_kernel(bias_ref, q_ref, kv_ref, out_ref):
    rows = q_ref.shape[0]
    inner = q_ref.shape[1]
    keys = kv_ref.shape[0]
    bias = bias_ref[...]
    lane = lax.broadcasted_iota(jnp.int32, (rows, 128), 1)
    low = lane < 64
    ones = jnp.ones((keys, 128), jnp.bfloat16)
    stats = jnp.zeros((rows, 128), jnp.float32)
    for pair in range(HEADS // 2):
        cols = slice(pair * 128, pair * 128 + 128)
        q_pair = q_ref[:, cols]
        k_pair = kv_ref[:, cols]
        v_ext = jnp.concatenate(
            [kv_ref[:, inner + pair * 128 : inner + pair * 128 + 128], ones], axis=1
        )
        parts = []
        for side in range(2):
            head = 2 * pair + side
            mine = low if side == 0 else jnp.logical_not(low)
            q_head = jnp.where(mine, q_pair, jnp.zeros_like(q_pair))
            scores = lax.dot_general(
                q_head, k_pair, (((1,), (1,)), ((), ())), preferred_element_type=jnp.float32
            )
            scores = scores + bias
            top = jnp.max(scores, axis=-1, keepdims=True)
            weights = jnp.exp(scores - top).astype(jnp.bfloat16)
            product = jnp.dot(weights, v_ext, preferred_element_type=jnp.float32)
            total = product[:, 128:]
            parts.append(product[:, :128] / total)
            lse = top + jnp.log(total)
            stats = jnp.where((lane & 7) == head, lse, stats)
        out_ref[:, cols] = jnp.where(low, parts[0], parts[1]).astype(jnp.bfloat16)
    high = stats.astype(jnp.bfloat16).astype(jnp.float32)
    rest = stats - high
    mid = rest.astype(jnp.bfloat16).astype(jnp.float32)
    packed = jnp.where(lane < 8, high, jnp.where(lane < 16, mid, rest - mid))
    out_ref[:, inner:] = packed.astype(jnp.bfloat16)


def attend(bias, queries, kv):
    count, inner = queries.shape
    keys = kv.shape[0]
    block = 512
    return pl.pallas_call(
        attend_kernel,
        grid=(count // block,),
        in_specs=[
            pl.BlockSpec((1, keys), lambda i: (0, 0)),
            pl.BlockSpec((block, inner), lambda i: (i, 0)),
            pl.BlockSpec((keys, 2 * inner), lambda i: (0, 0)),
        ],
        out_specs=pl.BlockSpec((block, inner + 128), lambda i: (i, 0)),
        out_shape=jax.ShapeDtypeStruct((count, inner + 128), jnp.bfloat16),
        compiler_params=pltpu.CompilerParams(vmem_limit_bytes=60 * 1024 * 1024),
    )(bias, queries, kv)


Z_SIZE = 8
KV_GROUPS = [[y * 16 + z * 2 + x for z in range(8)] for y in range(4) for x in range(2)]
Q_GROUPS = [[y * 16 + z * 2 + x for y in range(4) for x in range(2)] for z in range(8)]


def per_device(frames, lengths, w_qkv, w_out, w_pw1, conv_taps, w_pw2):
    stream = frames[0]
    frame_rows = stream.shape[0]
    my_index = lax.axis_index("ctx")
    my_start = my_index * frame_rows
    limit = lengths[0]
    positions = my_start + jnp.arange(frame_rows, dtype=jnp.int32)
    valid = positions < limit
    normed = to_bf16(layer_norm(stream.astype(jnp.float32)))
    projected = jnp.dot(normed, w_qkv, preferred_element_type=jnp.float32)
    inner = w_out.shape[0]
    head_size = inner // HEADS
    queries = to_bf16(projected[:, :inner] * head_size ** (-0.5))
    kv = to_bf16(projected[:, inner:])
    kv_all = lax.all_gather(kv, "ctx", axis=0, tiled=True, axis_index_groups=KV_GROUPS)
    q_all = lax.all_gather(queries, "ctx", axis=0, tiled=True, axis_index_groups=Q_GROUPS)
    group_start = (my_index // 16) * 16 + my_index % 2
    key_rows = jnp.arange(Z_SIZE * frame_rows, dtype=jnp.int32)
    key_spots = (group_start + 2 * (key_rows // frame_rows)) * frame_rows + key_rows % frame_rows
    bias = jnp.where(key_spots < limit, 0.0, masked_score).astype(jnp.float32)[None]
    partial = attend(bias, q_all, kv_all)
    width = partial.shape[1]
    returned = lax.all_to_all(
        partial, "ctx", split_axis=0, concat_axis=0, tiled=True, axis_index_groups=Q_GROUPS
    ).reshape(8, frame_rows, width)
    stats = returned[:, :, inner : inner + 24].astype(jnp.float32)
    lse = stats[:, :, 0:8] + stats[:, :, 8:16] + stats[:, :, 16:24]
    share = jnp.exp(lse - jnp.max(lse, axis=0))
    share = share / jnp.sum(share, axis=0)
    share = jnp.repeat(share, head_size, axis=2)
    attended = to_bf16(jnp.sum(returned[:, :, :inner].astype(jnp.float32) * share, axis=0))
    first = to_bf16(
        stream.astype(jnp.float32) + jnp.dot(attended, w_out, preferred_element_type=jnp.float32)
    )
    half_width = conv_taps.shape[0] // 2
    gated_own = gate_rows(first, positions, limit, w_pw1)
    padded = padded_2(gated_own, (("ctx", 0),), half_width)
    conv = depthwise(padded, conv_taps, frame_rows)
    swished = to_bf16(jax.nn.silu(layer_norm(conv)))
    second = first.astype(jnp.float32) + jnp.dot(swished, w_pw2, preferred_element_type=jnp.float32)
    encoded = jnp.where(valid[:, None], layer_norm(second), 0.0).astype(jnp.bfloat16)
    return encoded[None]


def solution(mesh):
    in_specs = (P("dp", "ctx", None), P("dp"), P(), P(), P(), P(), P())
    out_specs = P("dp", "ctx", None)
    return jax.shard_map(
        per_device, mesh=mesh, in_specs=in_specs, out_specs=out_specs, check_vma=False
    )
```

```python
import jax
import jax.numpy as jnp
from jax import lax
from jax.experimental import pallas as pl
from jax.experimental.pallas import tpu as pltpu
from jax.sharding import PartitionSpec as P

HEADS = 8


epsilon = 1e-05
masked_score = -1e30


def padded_2(cells, sides, width):
    for axis, dim in sides:
        count = lax.axis_size(axis)
        ends = count - 1
        head = lax.slice_in_dim(cells, 0, width, axis=dim)
        tail = lax.slice_in_dim(cells, cells.shape[dim] - width, cells.shape[dim], axis=dim)
        cells = jnp.concatenate(
            [
                lax.ppermute(tail, axis, [(i, (i + 1) % count) for i in range(ends)]),
                cells,
                lax.ppermute(head, axis, [((i + 1) % count, i) for i in range(ends)]),
            ],
            axis=dim,
        )
    return cells


def to_bf16(value):
    return value.astype(jnp.bfloat16)


def layer_norm(value):
    center = value - jnp.mean(value, axis=-1, keepdims=True)
    spread = jnp.mean(center * center, axis=-1, keepdims=True)
    return center * lax.rsqrt(spread + epsilon)


def depthwise(padded, conv_taps, count):
    total = jnp.zeros((count, padded.shape[1]), jnp.float32)
    for tap_index in range(conv_taps.shape[0]):
        total = total + conv_taps[tap_index] * padded[tap_index : tap_index + count].astype(
            jnp.float32
        )
    return total


def gate_rows(stream_rows, spots, limit, w_pw1):
    gated = jnp.dot(
        to_bf16(layer_norm(stream_rows.astype(jnp.float32))),
        w_pw1,
        preferred_element_type=jnp.float32,
    )
    half_cols = gated.shape[1] // 2
    result = gated[:, :half_cols] * jax.nn.sigmoid(gated[:, half_cols:])
    return to_bf16(jnp.where((spots < limit)[:, None], result, 0.0))


def attend_kernel(bias_ref, q_ref, kv_ref, out_ref):
    rows = q_ref.shape[0]
    inner = q_ref.shape[1]
    keys = kv_ref.shape[0]
    bias = bias_ref[...]
    lane = lax.broadcasted_iota(jnp.int32, (rows, 128), 1)
    low = lane < 64
    ones = jnp.ones((keys, 128), jnp.bfloat16)
    stats = jnp.zeros((rows, 128), jnp.float32)
    for pair in range(HEADS // 2):
        cols = slice(pair * 128, pair * 128 + 128)
        q_pair = q_ref[:, cols]
        k_pair = kv_ref[:, cols]
        v_ext = jnp.concatenate(
            [kv_ref[:, inner + pair * 128 : inner + pair * 128 + 128], ones], axis=1
        )
        parts = []
        for side in range(2):
            head = 2 * pair + side
            mine = low if side == 0 else jnp.logical_not(low)
            q_head = jnp.where(mine, q_pair, jnp.zeros_like(q_pair))
            scores = lax.dot_general(
                q_head, k_pair, (((1,), (1,)), ((), ())), preferred_element_type=jnp.float32
            )
            scores = scores + bias
            top = jnp.max(scores, axis=-1, keepdims=True)
            weights = jnp.exp(scores - top).astype(jnp.bfloat16)
            product = jnp.dot(weights, v_ext, preferred_element_type=jnp.float32)
            total = product[:, 128:]
            parts.append(product[:, :128] / total)
            lse = top + jnp.log(total)
            stats = jnp.where((lane & 7) == head, lse, stats)
        out_ref[:, cols] = jnp.where(low, parts[0], parts[1]).astype(jnp.bfloat16)
    high = stats.astype(jnp.bfloat16).astype(jnp.float32)
    rest = stats - high
    mid = rest.astype(jnp.bfloat16).astype(jnp.float32)
    packed = jnp.where(lane < 8, high, jnp.where(lane < 16, mid, rest - mid))
    out_ref[:, inner:] = packed.astype(jnp.bfloat16)


def attend(bias, queries, kv):
    count, inner = queries.shape
    keys = kv.shape[0]
    block = 512
    return pl.pallas_call(
        attend_kernel,
        grid=(count // block,),
        in_specs=[
            pl.BlockSpec((1, keys), lambda i: (0, 0)),
            pl.BlockSpec((block, inner), lambda i: (i, 0)),
            pl.BlockSpec((keys, 2 * inner), lambda i: (0, 0)),
        ],
        out_specs=pl.BlockSpec((block, inner + 128), lambda i: (i, 0)),
        out_shape=jax.ShapeDtypeStruct((count, inner + 128), jnp.bfloat16),
        compiler_params=pltpu.CompilerParams(vmem_limit_bytes=60 * 1024 * 1024),
    )(bias, queries, kv)


def gather_kernel(q_ref, kv_ref, q_all, kv_all, q_send, q_recv, kv_send, kv_recv, own_sem):
    me = lax.axis_index("ctx")
    y, z, x = me // 16, (me // 2) % 8, me % 2
    mine = y * 2 + x
    rows = q_ref.shape[0]
    half = rows // 2

    def ring_peer(shift):
        return y * 16 + lax.rem(z + shift + 8, 8) * 2 + x

    def plane_peer(shift):
        spot = lax.rem(mine + shift, 8)
        return (spot // 2) * 16 + z * 2 + lax.rem(spot, 2)

    barrier = pltpu.get_barrier_semaphore()
    for peer in [ring_peer(1), ring_peer(-1)] + [plane_peer(j) for j in range(1, 8)]:
        pl.semaphore_signal(
            barrier, inc=1, device_id={"ctx": peer}, device_id_type=pl.DeviceIdType.MESH
        )
    pl.semaphore_wait(barrier, 9)

    def ring_copy(way, step, chunk):
        sign = 1 if way == 0 else -1
        slot = lax.rem(z - sign * (step - 1) + 8, 8)
        place = pl.ds(pl.multiple_of(slot * rows + chunk * half, half), half)
        source = kv_ref.at[pl.ds(chunk * half, half)] if step == 1 else kv_all.at[place]
        return pltpu.make_async_remote_copy(
            src_ref=source,
            dst_ref=kv_all.at[place],
            send_sem=kv_send.at[way, step - 1, chunk],
            recv_sem=kv_recv.at[way, step - 1, chunk],
            device_id={"ctx": ring_peer(sign)},
            device_id_type=pl.DeviceIdType.MESH,
        )

    ring = {}
    for chunk in range(2):
        for way in range(2):
            ring[way, 1, chunk] = ring_copy(way, 1, chunk)
            ring[way, 1, chunk].start()
    pushes = []
    q_place = pl.ds(pl.multiple_of(mine * rows, rows), rows)
    for j in range(1, 8):
        push = pltpu.make_async_remote_copy(
            src_ref=q_ref,
            dst_ref=q_all.at[q_place],
            send_sem=q_send.at[j],
            recv_sem=q_recv.at[j],
            device_id={"ctx": plane_peer(j)},
            device_id_type=pl.DeviceIdType.MESH,
        )
        push.start()
        pushes.append(push)
    own_q = pltpu.make_async_copy(q_ref, q_all.at[q_place], own_sem.at[0])
    own_q.start()
    kv_place = pl.ds(pl.multiple_of(z * rows, rows), rows)
    own_kv = pltpu.make_async_copy(kv_ref, kv_all.at[kv_place], own_sem.at[1])
    own_kv.start()
    for step in range(2, 5):
        for chunk in range(2):
            for way in range(2):
                ring[way, step - 1, chunk].wait_recv()
                if step < 4 or chunk == way:
                    ring[way, step, chunk] = ring_copy(way, step, chunk)
                    ring[way, step, chunk].start()
    for way in range(2):
        ring[way, 4, way].wait_recv()
    for copy in ring.values():
        copy.wait_send()
    for push in pushes:
        push.wait_send()
        push.wait_recv()
    own_q.wait()
    own_kv.wait()


def gather_both(queries, kv):
    rows, inner = queries.shape
    hbm = pl.BlockSpec(memory_space=pl.ANY)
    return pl.pallas_call(
        gather_kernel,
        in_specs=[hbm, hbm],
        out_specs=[hbm, hbm],
        out_shape=[
            jax.ShapeDtypeStruct((8 * rows, inner), jnp.bfloat16),
            jax.ShapeDtypeStruct((8 * rows, 2 * inner), jnp.bfloat16),
        ],
        scratch_shapes=[
            pltpu.SemaphoreType.DMA((8,)),
            pltpu.SemaphoreType.DMA((8,)),
            pltpu.SemaphoreType.DMA((2, 4, 2)),
            pltpu.SemaphoreType.DMA((2, 4, 2)),
            pltpu.SemaphoreType.DMA((2,)),
        ],
        compiler_params=pltpu.CompilerParams(collective_id=0, has_side_effects=True),
    )(queries, kv)


Z_SIZE = 8
Q_GROUPS = [[y * 16 + z * 2 + x for y in range(4) for x in range(2)] for z in range(8)]


def per_device(frames, lengths, w_qkv, w_out, w_pw1, conv_taps, w_pw2):
    stream = frames[0]
    frame_rows = stream.shape[0]
    my_index = lax.axis_index("ctx")
    my_start = my_index * frame_rows
    limit = lengths[0]
    positions = my_start + jnp.arange(frame_rows, dtype=jnp.int32)
    valid = positions < limit
    normed = to_bf16(layer_norm(stream.astype(jnp.float32)))
    projected = jnp.dot(normed, w_qkv, preferred_element_type=jnp.float32)
    inner = w_out.shape[0]
    head_size = inner // HEADS
    queries = to_bf16(projected[:, :inner] * head_size ** (-0.5))
    kv = to_bf16(projected[:, inner:])
    q_all, kv_all = gather_both(queries, kv)
    group_start = (my_index // 16) * 16 + my_index % 2
    key_rows = jnp.arange(Z_SIZE * frame_rows, dtype=jnp.int32)
    key_spots = (group_start + 2 * (key_rows // frame_rows)) * frame_rows + key_rows % frame_rows
    bias = jnp.where(key_spots < limit, 0.0, masked_score).astype(jnp.float32)[None]
    partial = attend(bias, q_all, kv_all)
    width = partial.shape[1]
    returned = lax.all_to_all(
        partial, "ctx", split_axis=0, concat_axis=0, tiled=True, axis_index_groups=Q_GROUPS
    ).reshape(8, frame_rows, width)
    stats = returned[:, :, inner : inner + 24].astype(jnp.float32)
    lse = stats[:, :, 0:8] + stats[:, :, 8:16] + stats[:, :, 16:24]
    share = jnp.exp(lse - jnp.max(lse, axis=0))
    share = share / jnp.sum(share, axis=0)
    share = jnp.repeat(share, head_size, axis=2)
    attended = to_bf16(jnp.sum(returned[:, :, :inner].astype(jnp.float32) * share, axis=0))
    first = to_bf16(
        stream.astype(jnp.float32) + jnp.dot(attended, w_out, preferred_element_type=jnp.float32)
    )
    half_width = conv_taps.shape[0] // 2
    gated_own = gate_rows(first, positions, limit, w_pw1)
    padded = padded_2(gated_own, (("ctx", 0),), half_width)
    conv = depthwise(padded, conv_taps, frame_rows)
    swished = to_bf16(jax.nn.silu(layer_norm(conv)))
    second = first.astype(jnp.float32) + jnp.dot(swished, w_pw2, preferred_element_type=jnp.float32)
    encoded = jnp.where(valid[:, None], layer_norm(second), 0.0).astype(jnp.bfloat16)
    return encoded[None]


def solution(mesh):
    in_specs = (P("dp", "ctx", None), P("dp"), P(), P(), P(), P(), P())
    out_specs = P("dp", "ctx", None)
    return jax.shard_map(
        per_device, mesh=mesh, in_specs=in_specs, out_specs=out_specs, check_vma=False
    )
```

```python
import jax
import jax.numpy as jnp
from jax import lax
from jax.experimental import pallas as pl
from jax.experimental.pallas import tpu as pltpu
from jax.sharding import PartitionSpec as P

HEADS = 8


epsilon = 1e-05
masked_score = -1e30


def padded_2(cells, sides, width):
    for axis, dim in sides:
        count = lax.axis_size(axis)
        ends = count - 1
        head = lax.slice_in_dim(cells, 0, width, axis=dim)
        tail = lax.slice_in_dim(cells, cells.shape[dim] - width, cells.shape[dim], axis=dim)
        cells = jnp.concatenate(
            [
                lax.ppermute(tail, axis, [(i, (i + 1) % count) for i in range(ends)]),
                cells,
                lax.ppermute(head, axis, [((i + 1) % count, i) for i in range(ends)]),
            ],
            axis=dim,
        )
    return cells


def to_bf16(value):
    return value.astype(jnp.bfloat16)


def layer_norm(value):
    center = value - jnp.mean(value, axis=-1, keepdims=True)
    spread = jnp.mean(center * center, axis=-1, keepdims=True)
    return center * lax.rsqrt(spread + epsilon)


def depthwise(padded, conv_taps, count):
    total = jnp.zeros((count, padded.shape[1]), jnp.float32)
    for tap_index in range(conv_taps.shape[0]):
        total = total + conv_taps[tap_index] * padded[tap_index : tap_index + count].astype(
            jnp.float32
        )
    return total


def gate_rows(stream_rows, spots, limit, w_pw1):
    gated = jnp.dot(
        to_bf16(layer_norm(stream_rows.astype(jnp.float32))),
        w_pw1,
        preferred_element_type=jnp.float32,
    )
    half_cols = gated.shape[1] // 2
    result = gated[:, :half_cols] * jax.nn.sigmoid(gated[:, half_cols:])
    return to_bf16(jnp.where((spots < limit)[:, None], result, 0.0))


def attend_rows(bias_ref, q_ref, kv_ref, out_ref):
    rows = q_ref.shape[0]
    inner = q_ref.shape[1]
    keys = kv_ref.shape[0]
    bias = bias_ref[...]
    lane = lax.broadcasted_iota(jnp.int32, (rows, 128), 1)
    low = lane < 64
    ones = jnp.ones((keys, 128), jnp.bfloat16)
    stats = jnp.zeros((rows, 128), jnp.float32)
    for pair in range(HEADS // 2):
        cols = slice(pair * 128, pair * 128 + 128)
        q_pair = q_ref[:, cols]
        k_pair = kv_ref[:, cols]
        v_ext = jnp.concatenate(
            [kv_ref[:, inner + pair * 128 : inner + pair * 128 + 128], ones], axis=1
        )
        parts = []
        for side in range(2):
            head = 2 * pair + side
            mine = low if side == 0 else jnp.logical_not(low)
            q_head = jnp.where(mine, q_pair, jnp.zeros_like(q_pair))
            scores = lax.dot_general(
                q_head, k_pair, (((1,), (1,)), ((), ())), preferred_element_type=jnp.float32
            )
            scores = scores + bias
            top = jnp.max(scores, axis=-1, keepdims=True)
            weights = jnp.exp(scores - top).astype(jnp.bfloat16)
            product = jnp.dot(weights, v_ext, preferred_element_type=jnp.float32)
            total = product[:, 128:]
            parts.append(product[:, :128] / total)
            lse = top + jnp.log(total)
            stats = jnp.where((lane & 7) == head, lse, stats)
        out_ref[:, cols] = jnp.where(low, parts[0], parts[1]).astype(jnp.bfloat16)
    high = stats.astype(jnp.bfloat16).astype(jnp.float32)
    rest = stats - high
    mid = rest.astype(jnp.bfloat16).astype(jnp.float32)
    packed = jnp.where(lane < 8, high, jnp.where(lane < 16, mid, rest - mid))
    out_ref[:, inner:] = packed.astype(jnp.bfloat16)


def attend_kernel(bias_ref, q_ref, kv_ref, back_ref, held, send_sem, recv_sem, own_sem):
    step = pl.program_id(0)
    me = lax.axis_index("ctx")
    y, z, x = me // 16, (me // 2) % 8, me % 2
    mine = y * 2 + x
    rows = back_ref.shape[0] // 8

    @pl.when(step == 0)
    def _():
        barrier = pltpu.get_barrier_semaphore()
        for j in range(1, 8):
            spot = lax.rem(mine + j, 8)
            peer = (spot // 2) * 16 + z * 2 + lax.rem(spot, 2)
            pl.semaphore_signal(
                barrier, inc=1, device_id={"ctx": peer}, device_id_type=pl.DeviceIdType.MESH
            )
        pl.semaphore_wait(barrier, 7)

    to_y = lax.rem(y + 1 + step, 4)
    q_rows = q_ref.at[pl.ds(pl.multiple_of(to_y * 2 * rows, 2 * rows), 2 * rows)]
    attend_rows(bias_ref, q_rows, kv_ref, held.at[step])
    place = pl.ds(pl.multiple_of(mine * rows, rows), rows)

    def push(at_step, to_x, flip):
        return pltpu.make_async_remote_copy(
            src_ref=held.at[at_step, pl.ds(pl.multiple_of(to_x * rows, rows), rows)],
            dst_ref=back_ref.at[place],
            send_sem=send_sem.at[at_step, flip],
            recv_sem=recv_sem.at[at_step, flip],
            device_id={"ctx": lax.rem(y + 1 + at_step, 4) * 16 + z * 2 + to_x},
            device_id_type=pl.DeviceIdType.MESH,
        )

    push(step, 1 - x, 1).start()

    @pl.when(step < 3)
    def _():
        push(step, x, 0).start()

    @pl.when(step == 3)
    def _():
        own = pltpu.make_async_copy(
            held.at[3, pl.ds(pl.multiple_of(x * rows, rows), rows)], back_ref.at[place], own_sem
        )
        own.start()
        for k in range(4):
            push(k, 1 - x, 1).wait()
            if k < 3:
                push(k, x, 0).wait()
        own.wait()


def attend(bias, queries, kv):
    count, inner = queries.shape
    keys = kv.shape[0]
    return pl.pallas_call(
        attend_kernel,
        grid=(4,),
        in_specs=[
            pl.BlockSpec((1, keys), lambda i: (0, 0)),
            pl.BlockSpec((count, inner), lambda i: (0, 0)),
            pl.BlockSpec((keys, 2 * inner), lambda i: (0, 0)),
        ],
        out_specs=pl.BlockSpec(memory_space=pl.ANY),
        out_shape=jax.ShapeDtypeStruct((count, inner + 128), jnp.bfloat16),
        scratch_shapes=[
            pltpu.VMEM((4, count // 4, inner + 128), jnp.bfloat16),
            pltpu.SemaphoreType.DMA((4, 2)),
            pltpu.SemaphoreType.DMA((4, 2)),
            pltpu.SemaphoreType.DMA,
        ],
        compiler_params=pltpu.CompilerParams(
            collective_id=1, has_side_effects=True, vmem_limit_bytes=60 * 1024 * 1024
        ),
    )(bias, queries, kv)


def gather_kernel(q_ref, kv_ref, q_all, kv_all, q_send, q_recv, kv_send, kv_recv, own_sem):
    me = lax.axis_index("ctx")
    y, z, x = me // 16, (me // 2) % 8, me % 2
    mine = y * 2 + x
    rows = q_ref.shape[0]
    half = rows // 2

    def ring_peer(shift):
        return y * 16 + lax.rem(z + shift + 8, 8) * 2 + x

    def plane_peer(shift):
        spot = lax.rem(mine + shift, 8)
        return (spot // 2) * 16 + z * 2 + lax.rem(spot, 2)

    barrier = pltpu.get_barrier_semaphore()
    for peer in [ring_peer(1), ring_peer(-1)] + [plane_peer(j) for j in range(1, 8)]:
        pl.semaphore_signal(
            barrier, inc=1, device_id={"ctx": peer}, device_id_type=pl.DeviceIdType.MESH
        )
    pl.semaphore_wait(barrier, 9)

    def ring_copy(way, step, chunk):
        sign = 1 if way == 0 else -1
        slot = lax.rem(z - sign * (step - 1) + 8, 8)
        place = pl.ds(pl.multiple_of(slot * rows + chunk * half, half), half)
        source = kv_ref.at[pl.ds(chunk * half, half)] if step == 1 else kv_all.at[place]
        return pltpu.make_async_remote_copy(
            src_ref=source,
            dst_ref=kv_all.at[place],
            send_sem=kv_send.at[way, step - 1, chunk],
            recv_sem=kv_recv.at[way, step - 1, chunk],
            device_id={"ctx": ring_peer(sign)},
            device_id_type=pl.DeviceIdType.MESH,
        )

    ring = {}
    for chunk in range(2):
        for way in range(2):
            ring[way, 1, chunk] = ring_copy(way, 1, chunk)
            ring[way, 1, chunk].start()
    pushes = []
    q_place = pl.ds(pl.multiple_of(mine * rows, rows), rows)
    for j in range(1, 8):
        push = pltpu.make_async_remote_copy(
            src_ref=q_ref,
            dst_ref=q_all.at[q_place],
            send_sem=q_send.at[j],
            recv_sem=q_recv.at[j],
            device_id={"ctx": plane_peer(j)},
            device_id_type=pl.DeviceIdType.MESH,
        )
        push.start()
        pushes.append(push)
    own_q = pltpu.make_async_copy(q_ref, q_all.at[q_place], own_sem.at[0])
    own_q.start()
    kv_place = pl.ds(pl.multiple_of(z * rows, rows), rows)
    own_kv = pltpu.make_async_copy(kv_ref, kv_all.at[kv_place], own_sem.at[1])
    own_kv.start()
    for step in range(2, 5):
        for chunk in range(2):
            for way in range(2):
                ring[way, step - 1, chunk].wait_recv()
                if step < 4 or chunk == way:
                    ring[way, step, chunk] = ring_copy(way, step, chunk)
                    ring[way, step, chunk].start()
    for way in range(2):
        ring[way, 4, way].wait_recv()
    for copy in ring.values():
        copy.wait_send()
    for push in pushes:
        push.wait_send()
        push.wait_recv()
    own_q.wait()
    own_kv.wait()


def gather_both(queries, kv):
    rows, inner = queries.shape
    hbm = pl.BlockSpec(memory_space=pl.ANY)
    return pl.pallas_call(
        gather_kernel,
        in_specs=[hbm, hbm],
        out_specs=[hbm, hbm],
        out_shape=[
            jax.ShapeDtypeStruct((8 * rows, inner), jnp.bfloat16),
            jax.ShapeDtypeStruct((8 * rows, 2 * inner), jnp.bfloat16),
        ],
        scratch_shapes=[
            pltpu.SemaphoreType.DMA((8,)),
            pltpu.SemaphoreType.DMA((8,)),
            pltpu.SemaphoreType.DMA((2, 4, 2)),
            pltpu.SemaphoreType.DMA((2, 4, 2)),
            pltpu.SemaphoreType.DMA((2,)),
        ],
        compiler_params=pltpu.CompilerParams(collective_id=0, has_side_effects=True),
    )(queries, kv)


Z_SIZE = 8


def per_device(frames, lengths, w_qkv, w_out, w_pw1, conv_taps, w_pw2):
    stream = frames[0]
    frame_rows = stream.shape[0]
    my_index = lax.axis_index("ctx")
    my_start = my_index * frame_rows
    limit = lengths[0]
    positions = my_start + jnp.arange(frame_rows, dtype=jnp.int32)
    valid = positions < limit
    normed = to_bf16(layer_norm(stream.astype(jnp.float32)))
    projected = jnp.dot(normed, w_qkv, preferred_element_type=jnp.float32)
    inner = w_out.shape[0]
    head_size = inner // HEADS
    queries = to_bf16(projected[:, :inner] * head_size ** (-0.5))
    kv = to_bf16(projected[:, inner:])
    q_all, kv_all = gather_both(queries, kv)
    group_start = (my_index // 16) * 16 + my_index % 2
    key_rows = jnp.arange(Z_SIZE * frame_rows, dtype=jnp.int32)
    key_spots = (group_start + 2 * (key_rows // frame_rows)) * frame_rows + key_rows % frame_rows
    bias = jnp.where(key_spots < limit, 0.0, masked_score).astype(jnp.float32)[None]
    returned = attend(bias, q_all, kv_all)
    returned = returned.reshape(8, frame_rows, returned.shape[1])
    stats = returned[:, :, inner : inner + 24].astype(jnp.float32)
    lse = stats[:, :, 0:8] + stats[:, :, 8:16] + stats[:, :, 16:24]
    share = jnp.exp(lse - jnp.max(lse, axis=0))
    share = share / jnp.sum(share, axis=0)
    share = jnp.repeat(share, head_size, axis=2)
    attended = to_bf16(jnp.sum(returned[:, :, :inner].astype(jnp.float32) * share, axis=0))
    first = to_bf16(
        stream.astype(jnp.float32) + jnp.dot(attended, w_out, preferred_element_type=jnp.float32)
    )
    half_width = conv_taps.shape[0] // 2
    gated_own = gate_rows(first, positions, limit, w_pw1)
    padded = padded_2(gated_own, (("ctx", 0),), half_width)
    conv = depthwise(padded, conv_taps, frame_rows)
    swished = to_bf16(jax.nn.silu(layer_norm(conv)))
    second = first.astype(jnp.float32) + jnp.dot(swished, w_pw2, preferred_element_type=jnp.float32)
    encoded = jnp.where(valid[:, None], layer_norm(second), 0.0).astype(jnp.bfloat16)
    return encoded[None]


def solution(mesh):
    in_specs = (P("dp", "ctx", None), P("dp"), P(), P(), P(), P(), P())
    out_specs = P("dp", "ctx", None)
    return jax.shard_map(
        per_device, mesh=mesh, in_specs=in_specs, out_specs=out_specs, check_vma=False
    )
```
